128 devices in a mesh: kt: 8 (over x_hi, z), ks: 16 (over y, x_lo, core).
Axes of the slice: x: 4 (x_hi: 2, x_lo: 2; x = x_hi * 2 + x_lo), y: 4, z: 4, core: 2. Of those that a mesh axis runs over, the one named last changes fastest.
Arguments:
- val_target: bfloat16 [16, 32, 512], P('kt', None, 'ks'), may hold values from -6 to 6
- cond_target: bfloat16 [16, 64, 512], P('kt', None, 'ks'), may hold values from -0.03125 to 0.03125
- val_source: bfloat16 [64, 32, 512], P('ks', None, 'kt'), may hold values from -6 to 6
- cond_source: bfloat16 [64, 64, 512], P('ks', None, 'kt'), may hold values from -0.125 to 0.125
- trial_vectors: bfloat16 [64, 16, 2048], P('ks', 'kt'), may hold values from -6 to 6
- screened: bfloat16 [512, 512, 512], P(None, ('kt', 'ks')), may hold values from -0.25 to 0.25
- pair_momentum: int32 [16, 64], replicated, may hold values from 0 to 511
Outputs:
- kernel_out: float32 [16, 16, 2048], P('kt', 'ks')
The draws below stay inside these ranges and needn't reach their ends.
All inputs are finite; a program needn't handle non-finite values.
Results may differ from the reference program's by a relative error of at most 0.019.
Values may be sent and summed in bfloat16 or wider, within the bound.
No kernel may reach another device: no remote copies, remote signals or barrier semaphores. Data moves between devices by JAX's collectives and lax.ppermute only.
A program may use at most 128 MiB of HBM per device.

```python
import jax
import jax.numpy as jnp
from jax import lax

NAUX = 512
NV = 32
NC = 64
NVEC = 16
NQ = 512
NKT = 16
NKS = 64


def plant(drawn, own_key, low, top_value):
    spot = [jax.random.randint(jax.random.fold_in(own_key, axis), (), 0, length) for axis, length in enumerate(drawn.shape)]
    longest = drawn.shape.index(max(drawn.shape))
    next_to = spot[:longest] + [(spot[longest] + 1) % drawn.shape[longest]] + spot[longest + 1:]
    return drawn.at[tuple(spot)].set(low).at[tuple(next_to)].set(top_value)


def block_levels(rng, shape, cuts, least, high):
    def one(axis_at, parts):
        heights = jax.random.uniform(jax.random.fold_in(jax.random.fold_in(rng, 6), axis_at), (parts,), jnp.float32, least / len(cuts), high / len(cuts))
        return jnp.repeat(jnp.exp(heights), shape[axis_at] // parts).reshape((-1,) + (1,) * (len(shape) - axis_at - 1))

    gain = one(*cuts[0])
    for cut in cuts[1:]:
        gain = gain * one(*cut)
    return gain


def bell_draw(rng, extent, width, reach, pieces=(), kind=jnp.bfloat16):
    factor_of = block_levels(rng, extent, pieces, -0.22, 0.18) if pieces else 1.0
    drawn = jax.random.normal(rng, extent, jnp.float32) * width * factor_of
    return jnp.minimum(jnp.maximum(drawn, -reach), reach).astype(kind)


def setup_inputs(seed: int = 0) -> dict:
    key_list = jax.random.split(jax.random.key(seed), 8)
    return {
        "val_target": bell_draw(key_list[0], (NKT, NV, NAUX), 1.0, 6.0, ((0, 8), (2, 16))),
        "cond_target": bell_draw(key_list[1], (NKT, NC, NAUX), (NAUX * NKS) ** -0.5, 0.03125, ((0, 8), (2, 16))),
        "val_source": bell_draw(key_list[2], (NKS, NV, NAUX), 1.0, 6.0, ((0, 16), (2, 8))),
        "cond_source": bell_draw(key_list[3], (NKS, NC, NAUX), (NC * NV) ** -0.5, 0.125, ((0, 16), (2, 8))),
        "trial_vectors": bell_draw(key_list[4], (NKS, NVEC, NV * NC), 1.0, 6.0, ((0, 16), (1, 8))),
        "screened": bell_draw(key_list[5], (NQ, NAUX, NAUX), NAUX ** -0.5, 0.25, ((1, 128),)),
        "pair_momentum": plant(jax.random.randint(key_list[6], (NKT, NKS), 0, NQ), jax.random.fold_in(key_list[6], 1), 0, NQ - 1).astype(jnp.int32),
    }


def reference(val_target, cond_target, val_source, cond_source, trial_vectors, screened, pair_momentum):
    highest = lax.Precision.HIGHEST
    trial_four = trial_vectors.reshape(NKS, NVEC, NV, NC).astype(jnp.float32)
    dressed = jnp.einsum("snwc,scq->snwq", trial_four, cond_source.astype(jnp.float32), precision=highest)
    dressed = dressed.astype(jnp.bfloat16).astype(jnp.float32)

    def one_target(index):
        momentum = pair_momentum[index]
        kernel_mats = screened[momentum].astype(jnp.float32)
        target_val = val_target[index].astype(jnp.float32)
        pair_prod = (target_val[None, :, None, :] * val_source.astype(jnp.float32)[:, None, :, :]).astype(jnp.bfloat16)
        kernels = jnp.einsum("svwp,spq->svwq", pair_prod.astype(jnp.float32), kernel_mats, precision=highest)
        kernels = kernels.astype(jnp.bfloat16).astype(jnp.float32)
        reduced = jnp.einsum("svwq,snwq->vnq", kernels, dressed, precision=highest)
        reduced = reduced.astype(jnp.bfloat16).astype(jnp.float32)
        result = jnp.einsum("vnq,cq->nvc", reduced, cond_target[index].astype(jnp.float32), precision=highest)
        return result.reshape(NVEC, NV * NC)

    return lax.map(one_target, jnp.arange(NKT, dtype=jnp.int32))
```

```python
import jax
import jax.numpy as jnp
from jax import lax
from jax.experimental import pallas as pl
from jax.experimental.pallas import tpu as pltpu
from jax.sharding import Mesh
from jax.sharding import PartitionSpec as P

ALL = ("xh", "z", "y", "xl", "core")
X = ("xh", "xl")
KT = ("xh", "z")
YX = ("y", "xl")
BF = jnp.bfloat16
F32 = jnp.float32
VMEM_LIMIT = 56 * 1024 * 1024


def swap(x, axes, size, mask):
    return lax.ppermute(x, axes, [(i, i ^ mask) for i in range(size)])


def gathered(x, axes, size):
    return [x] + [swap(x, axes, size, k) for k in range(1, size)]


def flip_if(bit, x, axis):
    return jnp.where(bit == 1, jnp.flip(x, axis), x)


def pair_kernel(svt_ref, *refs):
    trial, outs = refs[:8], refs[8:]
    lane = lax.broadcasted_iota(jnp.int32, (64, 256), 1)
    first = (lane & 64) == 0
    for k in range(8):
        for sp in range(2):
            block = trial[k][sp]
            even = jnp.dot(svt_ref[2 * sp], block, preferred_element_type=F32)
            odd = jnp.dot(svt_ref[2 * sp + 1], block, preferred_element_type=F32)
            both = jnp.where(first, even, odd)
            for peer in range(8):
                rows = both[peer * 8 : peer * 8 + 8]
                piece = jnp.concatenate([rows[:, :128], rows[:, 128:]], axis=0)
                outs[peer][sp, k * 16 : k * 16 + 16, :] = piece.astype(BF)


def main_kernel(me_ref, pm_ref, w_ref, *refs):
    a_refs, pa, pb, pc = refs[:8], refs[8:12], refs[12:16], refs[16:20]
    out_ref, cs, ct, xs, acc = refs[20:]
    xh, z, y, xl, core = (me_ref[i] for i in range(5))
    kt, yx = xh * 4 + z, y * 2 + xl

    def where_from(rx, ry, rz):
        kt_from = kt ^ (((rx >> 1) << 2) | rz)
        yx_rel = (ry << 1) | (rx & 1)
        return kt_from, yx_rel

    def spread(block, rx, ry, rz, q_at, q_rows, ct_at):
        kt_from, yx_rel = where_from(rx, ry, rz)
        for sp in range(2):
            start = pl.multiple_of(kt_from * 64 + q_at, 16)
            cs[yx_rel, sp, pl.ds(start, q_rows), :] = block[sp * q_rows : (sp + 1) * q_rows]
        if ct_at is not None:
            for other in range(2):
                chip = ((yx_rel ^ yx) << 1) | (core ^ other)
                start = pl.multiple_of(chip * 32 + ct_at, 16)
                ct[kt_from, pl.ds(start, 16), :] = block[32 + 16 * other : 48 + 16 * other]

    for last in range(4):

        def one(i, carry, last=last):
            hi, lo = i >> 2, i & 3
            spread(pa[last][hi, lo], lo, hi, last, 0, 32, None)
            spread(pb[last][hi, lo], last, lo, hi, 32, 16, 0)
            spread(pc[last][hi, lo], hi, last, lo, 48, 16, 16)
            return carry

        lax.fori_loop(0, 16, one, 0)

    lane = lax.broadcasted_iota(jnp.int32, (128, 128), 1)
    first = lane < 64
    for chunk in range(4):
        for jj in range(2):
            j = chunk * 2 + jj
            for sp in range(2):
                a = a_refs[j][sp]
                none = jnp.zeros_like(a)
                lhs = jnp.concatenate([jnp.where(first, a, none), jnp.where(first, none, a)], axis=0)
                x = lax.dot_general(
                    lhs, cs[j, sp], (((1,), (1,)), ((), ())), preferred_element_type=F32
                ).astype(BF)
                xs[(jj * 2 + sp) * 2] = x[:128]
                xs[(jj * 2 + sp) * 2 + 1] = x[128:]

        def one_target(t, carry, chunk=chunk):
            mats = []
            for jj in range(2):
                source = (((chunk * 2 + jj) ^ yx) * 2 + core) * 4
                mats += [pm_ref[t, source + i] for i in range(4)]
            for qb in range(4):
                lanes = slice(qb * 128, qb * 128 + 128)
                w = [w_ref[m, :, lanes] for m in mats]
                for nb in range(8):
                    rows = slice(nb * 16, nb * 16 + 16)
                    terms = [w[i] * xs[i, rows, lanes] for i in range(8)]
                    while len(terms) > 1:
                        terms = [terms[i] + terms[i + 1] for i in range(0, len(terms), 2)]
                    total = terms[0].astype(F32)
                    if chunk > 0:
                        total = total + acc[t, rows, lanes]
                    acc[t, rows, lanes] = total
            return carry

        lax.fori_loop(0, 16, one_target, 0)

    def project(pair, carry):
        z0 = jnp.dot(acc[2 * pair].astype(BF), ct[pair], preferred_element_type=F32)
        z1 = jnp.dot(acc[2 * pair + 1].astype(BF), ct[pair], preferred_element_type=F32)
        zz = jnp.where(first, z0, z1).reshape(16, 8, 128).astype(BF)
        for k in range(8):
            n_at = (kt ^ k) * 2
            out_ref[pair, pl.ds(n_at, 2)] = zz[2 * k : 2 * k + 2]
        return carry

    lax.fori_loop(0, 8, project, 0)


def local(val_target, cond_target, val_source, cond_source, trial_vectors, screened, pair_momentum):
    xh, z, y, xl, core = (lax.axis_index(a) for a in ALL)
    me = jnp.stack([xh, z, y, xl, core, xh, xh, xh]).astype(jnp.int32)

    trial = trial_vectors.reshape(2, 2, 2, 32, 64).transpose(0, 3, 2, 1, 4).reshape(2, 32, 256)
    trials = gathered(trial, KT, 8)
    sv = val_source.reshape(4, 32, 2, 2, 2, 2, 4)
    sv = flip_if(y >> 1, sv, 2)
    sv = flip_if(y & 1, sv, 3)
    sv = flip_if(xl, sv, 4)
    sv = flip_if(core, sv, 5)
    svt = sv.reshape(4, 32, 64).transpose(0, 2, 1)

    other = swap(screened, "core", 2, 1)
    w_rep = jnp.concatenate([screened, other, screened, other], axis=1)

    cs = cond_source.reshape(2, 2, 64, 64).transpose(0, 3, 1, 2).reshape(2, 64, 128)
    ct = cond_target.transpose(2, 0, 1).reshape(32, 128)
    part_a = cs[:, :32].reshape(64, 128)
    part_b, ct_b = cs[:, 32:48].reshape(32, 128), ct[:16]
    part_c, ct_c = cs[:, 48:].reshape(32, 128), ct[16:]
    a1 = jnp.stack(gathered(part_a, X, 4))

    def with_other(part, extra, axis):
        own = gathered(jnp.concatenate([part, extra], axis=0), axis, 4)
        cross = [swap(extra, (axis, "core"), 8, 2 * k + 1) for k in range(4)]
        return jnp.stack([jnp.concatenate([o, c], axis=0) for o, c in zip(own, cross)])

    b1 = with_other(part_b, ct_b, "y")
    c1 = with_other(part_c, ct_c, "z")
    a2 = jnp.stack(gathered(a1, "y", 4))
    b2 = jnp.stack(gathered(b1, "z", 4))
    c2 = jnp.stack(gathered(c1, X, 4))
    a3, b3, c3 = gathered(a2, "z", 4), gathered(b2, X, 4), gathered(c2, "y", 4)

    vmem = pl.BlockSpec(memory_space=pltpu.VMEM)
    smem = pl.BlockSpec(memory_space=pltpu.SMEM)
    pieces = pl.pallas_call(
        pair_kernel,
        out_shape=[jax.ShapeDtypeStruct((2, 128, 128), BF)] * 8,
        in_specs=[vmem] * 9,
        out_specs=[vmem] * 8,
        compiler_params=pltpu.CompilerParams(vmem_limit_bytes=VMEM_LIMIT),
        name="pairs",
    )(svt, *trials)
    a = [pieces[0]] + [swap(pieces[k], YX, 8, k) for k in range(1, 8)]

    zs = pl.pallas_call(
        main_kernel,
        out_shape=jax.ShapeDtypeStruct((8, 16, 8, 128), BF),
        in_specs=[smem, smem] + [vmem] * 21,
        out_specs=vmem,
        scratch_shapes=[
            pltpu.VMEM((8, 2, 512, 128), BF),
            pltpu.VMEM((8, 512, 128), BF),
            pltpu.VMEM((8, 128, 512), BF),
            pltpu.VMEM((16, 128, 512), F32),
        ],
        compiler_params=pltpu.CompilerParams(vmem_limit_bytes=VMEM_LIMIT),
        name="screen",
    )(me, pair_momentum, w_rep, *a, *a3, *b3, *c3)

    tv = val_target.reshape(16, 128)
    tv = jnp.stack(gathered(tv, "core", 2))
    tv = jnp.stack(gathered(tv, "xl", 2))
    tv = jnp.stack(gathered(tv, "y", 4)).reshape(2, 2, 2, 2, 2, 32, 32)
    tv = flip_if(y >> 1, tv, 0)
    tv = flip_if(y & 1, tv, 1)
    tv = flip_if(xl, tv, 2)
    tv = flip_if(core, tv, 3)
    tv = tv.reshape(16, 2, 32, 32).transpose(1, 2, 0, 3).reshape(2, 32, 64, 2, 4)
    tv = jnp.stack([tv, jnp.flip(tv, 3)], axis=3).reshape(64, 1024)

    arrived = lax.all_to_all(zs.reshape(128, 8, 128), ALL, split_axis=0, concat_axis=0, tiled=True)
    result = jnp.dot(tv, arrived.reshape(1024, 128), preferred_element_type=F32)
    result = result.reshape(2, 32, 2, 64)
    result = jnp.stack([result[0, :, 0], result[1, :, 1]])
    return result.reshape(2, 1, 2048)


def solution(mesh):
    fine = Mesh(mesh.devices.reshape(2, 4, 4, 2, 2), ALL)
    kt, ks = ("xh", "z"), ("y", "xl", "core")
    in_specs = (
        P(kt, None, ks),
        P(kt, None, ks),
        P(ks, None, kt),
        P(ks, None, kt),
        P(ks, kt, None),
        P(None, kt + ks, None),
        P(),
    )
    return jax.shard_map(local, mesh=fine, in_specs=in_specs, out_specs=P(kt, ks, None), check_vma=False)
```

```python
import jax
import jax.numpy as jnp
from jax import lax
from jax.experimental import pallas as pl
from jax.experimental.pallas import tpu as pltpu
from jax.sharding import Mesh
from jax.sharding import PartitionSpec as P

ALL = ("xh", "z", "y", "xl", "core")
YX = ("y", "xl")
KT = ("xh", "z")
CHIPS = ("xh", "z", "y", "xl")
CS, CT, TV, ROWS = 256, 1280, 1536, 1552
BF = jnp.bfloat16
F32 = jnp.float32
VMEM_LIMIT = 24 * 1024 * 1024


def swap(x, axes, size, mask):
    return lax.ppermute(x, axes, [(i, i ^ mask) for i in range(size)])


def flip_if(bit, x, axis):
    return jnp.where(bit == 1, jnp.flip(x, axis), x)


def pair_kernel(svt_ref, first_ref, tv_ref, out_ref):
    lane = lax.broadcasted_iota(jnp.int32, (64, 256), 1)
    even_s = (lane & 64) == 0
    for k in range(8):
        for sp in range(2):
            at = sp * 32
            block = jnp.concatenate([first_ref[k, at : at + 32], first_ref[k, 64 + at : 96 + at]], axis=1)
            even = jnp.dot(svt_ref[2 * sp], block, preferred_element_type=F32)
            odd = jnp.dot(svt_ref[2 * sp + 1], block, preferred_element_type=F32)
            both = jnp.where(even_s, even, odd)
            for peer in range(8):
                rows = both[peer * 8 : peer * 8 + 8]
                piece = jnp.concatenate([rows[:, :128], rows[:, 128:]], axis=0)
                at = sp * 128 + k * 16
                out_ref[peer, at : at + 16, :] = piece.astype(BF)
            factors = first_ref[k, 128 + sp * 64 : 192 + sp * 64]
            for peer in range(8):
                at = CS + sp * 512 + k * 64
                out_ref[peer, at : at + 64, :] = factors
        factors = first_ref[k, 256:288]
        for peer in range(8):
            out_ref[peer, CT + k * 32 : CT + k * 32 + 32, :] = factors
    for peer in range(8):
        out_ref[peer, TV:ROWS, :] = tv_ref[...]


def repeat_kernel(own_ref, other_ref, out_ref):
    eight = jnp.concatenate([own_ref[...], other_ref[...]], axis=1)
    out_ref[...] = jnp.concatenate([eight, eight], axis=1)


def screen_kernel(core_ref, pm_ref, w_hbm, all_ref, out_ref, w_ref, xs, acc, sem):
    fetch = pltpu.make_async_copy(w_hbm, w_ref, sem)
    fetch.start()
    core = core_ref[0]
    lane = lax.broadcasted_iota(jnp.int32, (128, 128), 1)
    first = lane < 64

    def one_chip(yx, carry):
        for sp in range(2):
            a = all_ref[yx, sp * 128 : sp * 128 + 128]
            none = jnp.zeros_like(a)
            lhs = jnp.concatenate([jnp.where(first, a, none), jnp.where(first, none, a)], axis=0)
            rhs = all_ref[yx, CS + sp * 512 : CS + sp * 512 + 512]
            x = lax.dot_general(
                lhs, rhs, (((1,), (1,)), ((), ())), preferred_element_type=F32
            ).astype(BF)
            xs[yx * 4 + sp * 2] = x[:128]
            xs[yx * 4 + sp * 2 + 1] = x[128:]
        return carry

    lax.fori_loop(0, 8, one_chip, 0)
    fetch.wait()
    for chunk in range(4):

        def one_target(t, carry, chunk=chunk):
            mats = []
            for jj in range(2):
                source = ((chunk * 2 + jj) * 2 + core) * 4
                mats += [pm_ref[t, source + i] for i in range(4)]
            for qb in range(4):
                lanes = slice(qb * 128, qb * 128 + 128)
                w = [w_ref[m, :, lanes] for m in mats]
                for nb in range(8):
                    rows = slice(nb * 16, nb * 16 + 16)
                    terms = [w[i] * xs[chunk * 8 + i, rows, lanes] for i in range(8)]
                    while len(terms) > 1:
                        terms = [terms[i] + terms[i + 1] for i in range(0, len(terms), 2)]
                    total = terms[0].astype(F32)
                    if chunk > 0:
                        total = total + acc[t, rows, lanes]
                    if chunk < 3:
                        acc[t, rows, lanes] = total
                    else:
                        out_ref[t, rows, lanes] = total.astype(BF)
            return carry

        lax.fori_loop(0, 16, one_target, 0)


def project_kernel(core_ref, y_ref, all_ref, other_ref, keep_ref, give_ref, ct):
    core = core_ref[0]
    lane = lax.broadcasted_iota(jnp.int32, (128, 128), 1)
    first = lane < 64

    def project(kt, carry):
        for yx in range(8):
            ct[pl.ds(pl.multiple_of((yx * 2 + core) * 32, 32), 32), :] = all_ref[
                yx, pl.ds(pl.multiple_of(CT + kt * 32, 32), 32), :
            ]
            ct[pl.ds(pl.multiple_of((yx * 2 + 1 - core) * 32, 32), 32), :] = other_ref[
                yx, pl.ds(pl.multiple_of(kt * 32, 32), 32), :
            ]
        c = ct[...]
        z0 = jnp.dot(y_ref[2 * kt], c, preferred_element_type=F32)
        z1 = jnp.dot(y_ref[2 * kt + 1], c, preferred_element_type=F32)
        zz = jnp.where(first, z0, z1).reshape(8, 2, 8, 128)
        keep_ref[kt] = jnp.where(core == 0, zz[:, 0], zz[:, 1]).astype(BF)
        give = jnp.where(core == 0, zz[:, 1], zz[:, 0])
        give_ref[kt] = jnp.concatenate([give[:, 4:], give[:, :4]], axis=1).astype(BF)
        return carry

    lax.fori_loop(0, 8, project, 0)


def local(val_target, cond_target, val_source, cond_source, trial_vectors, screened, pair_momentum):
    core = lax.axis_index("core")
    me = core.astype(jnp.int32).reshape(1)
    vmem = pl.BlockSpec(memory_space=pltpu.VMEM)
    smem = pl.BlockSpec(memory_space=pltpu.SMEM)
    params = pltpu.CompilerParams(vmem_limit_bytes=VMEM_LIMIT)

    def all_to_all(x, axes):
        return lax.all_to_all(x, axes, split_axis=0, concat_axis=0, tiled=True)

    trial = trial_vectors.reshape(2, 2, 2, 32, 64).transpose(2, 0, 3, 1, 4).reshape(128, 128)
    cs = cond_source.reshape(2, 2, 64, 64).transpose(0, 3, 1, 2).reshape(128, 128)
    ct = cond_target.transpose(2, 0, 1).reshape(32, 128)
    block = jnp.concatenate([trial, cs, ct], axis=0)
    near = all_to_all(jnp.broadcast_to(block[None], (8, 288, 128)), KT)

    other = swap(screened, "core", 2, 1)
    w_rows = pl.pallas_call(
        repeat_kernel,
        out_shape=jax.ShapeDtypeStruct((512, 16, 512), BF),
        grid=(8,),
        in_specs=[pl.BlockSpec((64, 4, 512), lambda i: (i, 0, 0))] * 2,
        out_specs=pl.BlockSpec((64, 16, 512), lambda i: (i, 0, 0)),
        compiler_params=params,
        name="rows",
    )(screened, other)
    near, w_rows = lax.optimization_barrier((near, w_rows))

    sv = flip_if(core, val_source.reshape(4, 32, 8, 2, 4), 3)
    svt = sv.reshape(4, 32, 64).transpose(0, 2, 1)
    pieces = pl.pallas_call(
        pair_kernel,
        out_shape=jax.ShapeDtypeStruct((8, ROWS, 128), BF),
        in_specs=[vmem] * 3,
        out_specs=vmem,
        compiler_params=params,
        name="pairs",
    )(svt, near, val_target.reshape(16, 128))
    every = all_to_all(pieces, YX)

    ys = pl.pallas_call(
        screen_kernel,
        out_shape=jax.ShapeDtypeStruct((16, 128, 512), BF),
        in_specs=[smem, smem, pl.BlockSpec(memory_space=pltpu.HBM), vmem],
        out_specs=vmem,
        scratch_shapes=[
            pltpu.VMEM((512, 16, 512), BF),
            pltpu.VMEM((32, 128, 512), BF),
            pltpu.VMEM((16, 128, 512), F32),
            pltpu.SemaphoreType.DMA,
        ],
        compiler_params=params,
        name="screen",
    )(me, pair_momentum, w_rows, every)
    ct_other = swap(every[:, CT:TV], "core", 2, 1)
    keep, give = pl.pallas_call(
        project_kernel,
        out_shape=[jax.ShapeDtypeStruct((8, 8, 8, 128), BF)] * 2,
        in_specs=[smem, vmem, vmem, vmem],
        out_specs=[vmem, vmem],
        scratch_shapes=[pltpu.VMEM((512, 128), BF)],
        compiler_params=params,
        name="project",
    )(me, ys, every, ct_other)
    taken = swap(give, "core", 2, 1)
    zs = (keep.astype(F32) + taken.astype(F32)).astype(BF)

    tv = every[:, TV:]
    tv_other = swap(tv, "core", 2, 1).reshape(8, 2, 32, 32)
    tv = tv.reshape(8, 2, 32, 32)
    tv = jnp.where(core == 0, jnp.stack([tv, tv_other], axis=1), jnp.stack([tv_other, tv], axis=1))
    tv = tv.transpose(2, 3, 0, 1, 4).reshape(2, 32, 64, 2, 4)
    tv = flip_if(core, tv, 3).reshape(64, 512)

    arrived = all_to_all(zs.reshape(64, 8, 128), CHIPS)
    result = jnp.dot(tv, arrived.reshape(512, 128), preferred_element_type=F32)
    result = result.reshape(2, 32, 2, 64)
    result = jnp.stack([result[0, :, 0], result[1, :, 1]])
    return result.reshape(2, 1, 2048)


def solution(mesh):
    fine = Mesh(mesh.devices.reshape(2, 4, 4, 2, 2), ALL)
    kt, ks = ("xh", "z"), ("y", "xl", "core")
    in_specs = (
        P(kt, None, ks),
        P(kt, None, ks),
        P(ks, None, kt),
        P(ks, None, kt),
        P(ks, kt, None),
        P(None, kt + ks, None),
        P(),
    )
    return jax.shard_map(local, mesh=fine, in_specs=in_specs, out_specs=P(kt, ks, None), check_vma=False)
```

```python
import functools

import jax
import jax.numpy as jnp
from jax import lax
from jax.experimental import pallas as pl
from jax.experimental.pallas import tpu as pltpu
from jax.sharding import Mesh
from jax.sharding import PartitionSpec as P

ALL = ("xh", "z", "y", "xl", "core")
YX = ("y", "xl")
KT = ("xh", "z")
X = ("xh", "xl")
CHIPS = ("xh", "z", "y", "xl")
BF = jnp.bfloat16
F32 = jnp.float32
VMEM_LIMIT = 8 * 1024 * 1024
NEAR = 48
TV = 256 + 16 * NEAR


def swap(x, axes, size, mask):
    return lax.ppermute(x, axes, [(i, i ^ mask) for i in range(size)])


def flip_if(bit, x, axis):
    return jnp.where(bit == 1, jnp.flip(x, axis), x)


def doubled(x, axes, size, mask):
    return jnp.concatenate([x, swap(x, axes, size, mask)], axis=0)


def cost(flops, bytes_accessed):
    return pl.CostEstimate(flops=flops, bytes_accessed=bytes_accessed, transcendentals=0)


def pair_kernel(svt_ref, near_ref, tv_ref, out_ref):
    lane = lax.broadcasted_iota(jnp.int32, (64, 256), 1)
    even_s = (lane & 64) == 0
    for k in range(8):
        for sp in range(2):
            at = sp * 32
            block = jnp.concatenate([near_ref[k, at : at + 32], near_ref[k, 64 + at : 96 + at]], axis=1)
            even = jnp.dot(svt_ref[2 * sp], block, preferred_element_type=F32)
            odd = jnp.dot(svt_ref[2 * sp + 1], block, preferred_element_type=F32)
            both = jnp.where(even_s, even, odd)
            for peer in range(8):
                rows = both[peer * 8 : peer * 8 + 8]
                piece = jnp.concatenate([rows[:, :128], rows[:, 128:]], axis=0)
                at = sp * 128 + k * 16
                out_ref[peer, at : at + 16, :] = piece.astype(BF)
        for peer in range(8):
            at = 256 + k * 2 * NEAR
            out_ref[peer, at : at + 2 * NEAR, :] = near_ref[k, 128 : 128 + 2 * NEAR]
    for peer in range(8):
        out_ref[peer, TV : TV + 16, :] = tv_ref[...]


def far_index(kt_mask, yx_mask):
    y_mask, xh_mask = yx_mask >> 1, kt_mask >> 2
    place = (((yx_mask & 1) ^ xh_mask) << 2) | (y_mask ^ (y_mask >> 1))
    return kt_mask ^ ((kt_mask >> 1) & 1), place


def screen_kernel(me_ref, pm_ref, own_ref, other_ref, every_ref, far_ref, ct_other_ref, out_ref, w_ref, xs, acc, ct):
    here, yx_here, core = me_ref[0], me_ref[1], me_ref[2]

    def eight_mats(step, carry):
        own, other = own_ref[pl.ds(step * 8, 8)], other_ref[pl.ds(step * 8, 8)]
        for half in range(2):
            parts = []
            for qb in (2 * half, 2 * half + 1):
                lanes = slice(qb * 128, qb * 128 + 128)
                parts += [own[:, :, lanes], other[:, :, lanes]]
            w_ref[pl.ds(step * 8, 8), half] = jnp.concatenate(parts, axis=1)
        return carry

    lax.fori_loop(0, 64, eight_mats, 0)
    lane = lax.broadcasted_iota(jnp.int32, (128, 128), 1)
    first = lane < 64

    def one_chip(yx, carry):
        for sp in range(2):
            a = every_ref[yx, sp * 128 : sp * 128 + 128]
            none = jnp.zeros_like(a)
            lhs = jnp.concatenate([jnp.where(first, a, none), jnp.where(first, none, a)], axis=0)
            factors = []
            for kt in range(8):
                at = 256 + (kt * 2 + sp) * NEAR
                j, i = far_index(kt ^ here, yx ^ yx_here)
                rest = far_ref[j, i, sp * (64 - NEAR) : (sp + 1) * (64 - NEAR)]
                factors += [every_ref[yx, at : at + NEAR], rest]
            rhs = jnp.concatenate(factors, axis=0)
            x = lax.dot_general(lhs, rhs, (((1,), (1,)), ((), ())), preferred_element_type=F32)
            x = x.reshape(2, 16, 8, 512)
            for half in range(2):
                at = half * 256
                tile = jnp.concatenate([x[..., at : at + 128], x[..., at + 128 : at + 256]], axis=2)
                xs[pl.ds(yx * 4 + sp * 2, 2), half] = tile.astype(BF)
        return carry

    lax.fori_loop(0, 8, one_chip, 0)
    for chunk in range(4):

        def one_target(t, carry, chunk=chunk):
            mats = []
            for yx in (2 * chunk, 2 * chunk + 1):
                source = (yx * 2 + core) * 4
                mats += [pm_ref[t, source + j] for j in range(4)]
            for half in range(2):
                w = [w_ref[m, half] for m in mats]
                for n in range(16):
                    terms = [w[j] * xs[chunk * 8 + j, half, n] for j in range(8)]
                    while len(terms) > 1:
                        terms = [terms[j] + terms[j + 1] for j in range(0, len(terms), 2)]
                    total = terms[0].astype(F32)
                    rows = slice(n * 8, n * 8 + 8)
                    for qb in range(2):
                        lanes = slice(half * 256 + qb * 128, half * 256 + qb * 128 + 128)
                        part = total[qb * 8 : qb * 8 + 8]
                        if chunk > 0:
                            part = part + acc[t, rows, lanes]
                        acc[t, rows, lanes] = part
            return carry

        lax.fori_loop(0, 16, one_target, 0)

    def project(kt, carry):
        for yx in range(8):
            j, i = far_index(kt ^ here, yx ^ yx_here)
            ct[pl.ds(pl.multiple_of((yx * 2 + core) * 32, 32), 32), :] = far_ref[j, i, 128 - 2 * NEAR :]
            ct[pl.ds(pl.multiple_of((yx * 2 + 1 - core) * 32, 32), 32), :] = ct_other_ref[j, i]
        c = ct[...]
        z0 = jnp.dot(acc[2 * kt].astype(BF), c, preferred_element_type=F32)
        z1 = jnp.dot(acc[2 * kt + 1].astype(BF), c, preferred_element_type=F32)
        out_ref[kt] = jnp.where(first, z0, z1).reshape(16, 8, 128).astype(BF)
        return carry

    lax.fori_loop(0, 8, project, 0)


def local(val_target, cond_target, val_source, cond_source, trial_vectors, screened, pair_momentum):
    xh, z, y, xl, core = (lax.axis_index(a) for a in ALL)
    me = jnp.stack([xh * 4 + z, y * 2 + xl, core]).astype(jnp.int32)
    vmem = pl.BlockSpec(memory_space=pltpu.VMEM)
    smem = pl.BlockSpec(memory_space=pltpu.SMEM)
    params = pltpu.CompilerParams(vmem_limit_bytes=VMEM_LIMIT)

    def all_to_all(x, axes):
        return lax.all_to_all(x, axes, split_axis=0, concat_axis=0, tiled=True)

    other = swap(screened, "core", 2, 1)

    trial = trial_vectors.reshape(2, 2, 2, 32, 64).transpose(2, 0, 3, 1, 4).reshape(128, 128)
    cs = cond_source.reshape(2, 2, 64, 64).transpose(0, 3, 1, 2).reshape(2, 64, 128)
    sent = jnp.concatenate([trial, cs[:, :NEAR].reshape(2 * NEAR, 128)], axis=0)
    sent = jnp.broadcast_to(sent[None], (8, 128 + 2 * NEAR, 128))
    near = all_to_all(sent, KT)

    sv = flip_if(core, val_source.reshape(4, 32, 8, 2, 4), 3)
    svt = sv.reshape(4, 32, 64).transpose(0, 2, 1)
    ct = cond_target.transpose(2, 0, 1).reshape(32, 128)
    block = jnp.concatenate([cs[:, NEAR:].reshape(128 - 2 * NEAR, 128), ct], axis=0)[None]
    block = doubled(block, "y", 4, 1)
    block, svt = lax.optimization_barrier((block, svt))
    block = doubled(block, "y", 4, 3)
    block = doubled(block, X, 4, 1)[None]
    near, block = lax.optimization_barrier((near, block))

    pieces = pl.pallas_call(
        pair_kernel,
        out_shape=jax.ShapeDtypeStruct((8, TV + 16, 128), BF),
        in_specs=[vmem] * 3,
        out_specs=vmem,
        compiler_params=params,
        name="pairs",
    )(svt, near, val_target.reshape(16, 128))
    every = all_to_all(pieces, YX)

    block = doubled(block, "z", 4, 1)
    block = doubled(block, "z", 4, 3)
    far = doubled(block, X, 4, 3)
    ct_other = swap(far[:, :, 128 - 2 * NEAR :], "core", 2, 1)

    zs = pl.pallas_call(
        screen_kernel,
        out_shape=jax.ShapeDtypeStruct((8, 16, 8, 128), BF),
        in_specs=[smem, smem] + [vmem] * 5,
        out_specs=vmem,
        scratch_shapes=[
            pltpu.VMEM((512, 2, 16, 128), BF),
            pltpu.VMEM((32, 2, 16, 16, 128), BF),
            pltpu.VMEM((16, 128, 512), F32),
            pltpu.VMEM((512, 128), BF),
        ],
        compiler_params=pltpu.CompilerParams(vmem_limit_bytes=24 * 1024 * 1024),
        cost_estimate=cost(8_000_000_000, 16_000_000),
        name="screen",
    )(me, pair_momentum, screened, other, every, far, ct_other)

    tv = every[:, TV:]
    tv_other = swap(tv, "core", 2, 1).reshape(8, 2, 32, 32)
    tv = tv.reshape(8, 2, 32, 32)
    tv = jnp.where(core == 0, jnp.stack([tv, tv_other], axis=1), jnp.stack([tv_other, tv], axis=1))
    tv = tv.transpose(2, 3, 0, 1, 4).reshape(2, 32, 64, 2, 4)
    tv = jnp.stack([tv, jnp.flip(tv, 3)], axis=3).reshape(64, 1024)

    arrived = all_to_all(zs.reshape(128, 8, 128), ALL)
    result = jnp.dot(tv, arrived.reshape(1024, 128), preferred_element_type=F32)
    result = result.reshape(2, 32, 2, 64)
    result = jnp.stack([result[0, :, 0], result[1, :, 1]])
    return result.reshape(2, 1, 2048)


def solution(mesh):
    fine = Mesh(mesh.devices.reshape(2, 4, 4, 2, 2), ALL)
    kt, ks = ("xh", "z"), ("y", "xl", "core")
    in_specs = (
        P(kt, None, ks),
        P(kt, None, ks),
        P(ks, None, kt),
        P(ks, None, kt),
        P(ks, kt, None),
        P(None, kt + ks, None),
        P(),
    )
    return jax.shard_map(local, mesh=fine, in_specs=in_specs, out_specs=P(kt, ks, None), check_vma=False)
```

```python
import functools

import jax
import jax.numpy as jnp
from jax import lax
from jax.experimental import pallas as pl
from jax.experimental.pallas import tpu as pltpu
from jax.sharding import Mesh
from jax.sharding import PartitionSpec as P

ALL = ("xh", "z", "y", "xl", "core")
YX = ("y", "xl")
KT = ("xh", "z")
X = ("xh", "xl")
CHIPS = ("xh", "z", "y", "xl")
BF = jnp.bfloat16
F32 = jnp.float32
VMEM_LIMIT = 8 * 1024 * 1024
NEAR = 48
TV = 256 + 16 * NEAR


def swap(x, axes, size, mask):
    return lax.ppermute(x, axes, [(i, i ^ mask) for i in range(size)])


def flip_if(bit, x, axis):
    return jnp.where(bit == 1, jnp.flip(x, axis), x)


def doubled(x, axes, size, mask):
    return jnp.concatenate([x, swap(x, axes, size, mask)], axis=0)


def cost(flops, bytes_accessed):
    return pl.CostEstimate(flops=flops, bytes_accessed=bytes_accessed, transcendentals=0)


def prepare_kernel(trial_ref, cs_ref, ct_ref, sent_ref, block_ref):
    trial = trial_ref[...]
    for k in range(8):
        sent_ref[k, :128, :] = trial
    for sp in range(2):
        pair = jnp.concatenate([cs_ref[2 * sp], cs_ref[2 * sp + 1]], axis=0)
        turned = jnp.transpose(pair.astype(F32)).astype(BF)
        for k in range(8):
            sent_ref[k, 128 + sp * NEAR : 128 + (sp + 1) * NEAR, :] = turned[:NEAR]
        block_ref[sp * (64 - NEAR) : (sp + 1) * (64 - NEAR), :] = turned[NEAR:]
    block_ref[128 - 2 * NEAR :, :] = jnp.concatenate([ct_ref[0], ct_ref[1]], axis=1)


def pair_kernel(sv_ref, near_ref, tv_ref, out_ref):
    row = lax.broadcasted_iota(jnp.int32, (32, 32), 0)
    column = lax.broadcasted_iota(jnp.int32, (32, 32), 1)
    lane = lax.broadcasted_iota(jnp.int32, (32, 128), 1)
    parity = lax.broadcasted_iota(jnp.int32, (32, 128), 0) & 1
    mine = (lane >> 6) == parity
    factors = []
    for s in range(4):
        for odd in range(2):
            chosen = ((row >> 1) * 2 + odd == column).astype(F32).astype(BF)
            values = jnp.dot(chosen, sv_ref[s], preferred_element_type=F32)
            values = jnp.where(mine, jnp.concatenate([values, values], axis=1), 0.0)
            factors.append(jnp.transpose(values).astype(BF))
    low = lax.broadcasted_iota(jnp.int32, (128, 128), 1) < 64
    for k in range(8):
        for sp in range(2):
            parts = []
            for s in (2 * sp, 2 * sp + 1):
                block = near_ref[k, s * 32 : s * 32 + 32]
                parts += [jnp.dot(factors[2 * s + odd], block, preferred_element_type=F32) for odd in range(2)]
            crossed = pltpu.roll(jnp.where(low, parts[2], parts[1]), 64, 1)
            both = (jnp.where(low, parts[0], parts[3]) + crossed).reshape(2, 8, 8, 128)
            for peer in range(8):
                piece = jnp.concatenate([both[0, peer], both[1, peer]], axis=0)
                at = sp * 128 + k * 16
                out_ref[peer, at : at + 16, :] = piece.astype(BF)
        for peer in range(8):
            at = 256 + k * 2 * NEAR
            out_ref[peer, at : at + 2 * NEAR, :] = near_ref[k, 128 : 128 + 2 * NEAR]
    for peer in range(8):
        out_ref[peer, TV : TV + 16, :] = tv_ref[...]


def far_index(kt_mask, yx_mask):
    y_mask, xh_mask = yx_mask >> 1, kt_mask >> 2
    place = (((yx_mask & 1) ^ xh_mask) << 2) | (y_mask ^ (y_mask >> 1))
    return kt_mask ^ ((kt_mask >> 1) & 1), place


def chosen(near_ref, far_ref, j, i):
    return jnp.where(j < 4, near_ref[j & 3, i], far_ref[j & 3, i])


def screen_kernel(
    me_ref, pm_ref, own_hbm, other_hbm, every_ref, near_ref, far_ref, ct_near_ref, ct_far_ref, out_ref,
    own_ref, other_ref, w_ref, xs, acc, ys, ct, sems,
):
    here, yx_here, core = me_ref[0], me_ref[1], me_ref[2]
    pairs = ((own_hbm, own_ref), (other_hbm, other_ref))
    fetches = [pltpu.make_async_copy(a, b, sems.at[i]) for i, (a, b) in enumerate(pairs)]
    for fetch in fetches:
        fetch.start()

    def eight_mats(step, carry):
        own, other = own_ref[pl.ds(step * 8, 8)], other_ref[pl.ds(step * 8, 8)]
        for half in range(2):
            parts = []
            for qb in (2 * half, 2 * half + 1):
                lanes = slice(qb * 128, qb * 128 + 128)
                parts += [own[:, :, lanes], other[:, :, lanes]]
            w_ref[pl.ds(step * 8, 8), half] = jnp.concatenate(parts, axis=1)
        return carry

    lane = lax.broadcasted_iota(jnp.int32, (128, 128), 1)
    first = lane < 64

    def one_chip(yx, carry):
        for sp in range(2):
            a = every_ref[yx, sp * 128 : sp * 128 + 128]
            none = jnp.zeros_like(a)
            lhs = jnp.concatenate([jnp.where(first, a, none), jnp.where(first, none, a)], axis=0)
            factors = []
            for kt in range(8):
                at = 256 + (kt * 2 + sp) * NEAR
                j, i = far_index(kt ^ here, yx ^ yx_here)
                rest = chosen(near_ref, far_ref, j, i)[sp * (64 - NEAR) : (sp + 1) * (64 - NEAR)]
                factors += [every_ref[yx, at : at + NEAR], rest]
            rhs = jnp.concatenate(factors, axis=0)
            x = lax.dot_general(lhs, rhs, (((1,), (1,)), ((), ())), preferred_element_type=F32)
            x = x.reshape(2, 16, 8, 512)
            for half in range(2):
                at = half * 256
                tile = jnp.concatenate([x[..., at : at + 128], x[..., at + 128 : at + 256]], axis=2)
                xs[pl.ds(yx * 4 + sp * 2, 2), half] = tile.astype(BF)
        return carry

    lax.fori_loop(0, 8, one_chip, 0)
    for fetch in fetches:
        fetch.wait()
    lax.fori_loop(0, 64, eight_mats, 0)
    for chunk in range(4):

        def one_target(t, carry, chunk=chunk):
            mats = []
            for yx in (2 * chunk, 2 * chunk + 1):
                source = (yx * 2 + core) * 4
                mats += [pm_ref[t, source + j] for j in range(4)]
            for half in range(2):
                w = [w_ref[m, half] for m in mats]
                for two in range(8):
                    sums = []
                    for n in (2 * two, 2 * two + 1):
                        terms = [w[j] * xs[chunk * 8 + j, half, n] for j in range(8)]
                        while len(terms) > 1:
                            terms = [terms[j] + terms[j + 1] for j in range(0, len(terms), 2)]
                        sums.append(terms[0].astype(F32))
                    rows = slice(two * 16, two * 16 + 16)
                    for qb in range(2):
                        lanes = slice(half * 256 + qb * 128, half * 256 + qb * 128 + 128)
                        part = jnp.concatenate([x[qb * 8 : qb * 8 + 8] for x in sums], axis=0)
                        if chunk > 0:
                            part = part + acc[t, rows, lanes]
                        if chunk < 3:
                            acc[t, rows, lanes] = part
                        else:
                            ys[t, rows, lanes] = part.astype(BF)
            return carry

        lax.fori_loop(0, 16, one_target, 0, unroll=4)

    def project(kt, carry):
        for yx in range(8):
            j, i = far_index(kt ^ here, yx ^ yx_here)
            ct[pl.ds(pl.multiple_of((yx * 2 + core) * 32, 32), 32), :] = chosen(near_ref, far_ref, j, i)[128 - 2 * NEAR :]
            sibling = chosen(ct_near_ref, ct_far_ref, j, i)
            ct[pl.ds(pl.multiple_of((yx * 2 + 1 - core) * 32, 32), 32), :] = sibling
        c = ct[...]
        z0 = jnp.dot(ys[2 * kt], c, preferred_element_type=F32)
        z1 = jnp.dot(ys[2 * kt + 1], c, preferred_element_type=F32)
        out_ref[kt] = jnp.where(first, z0, z1).reshape(16, 8, 128).astype(BF)
        return carry

    lax.fori_loop(0, 8, project, 0)


def local(val_target, cond_target, val_source, cond_source, trial_vectors, screened, pair_momentum):
    xh, z, y, xl, core = (lax.axis_index(a) for a in ALL)
    me = jnp.stack([xh * 4 + z, y * 2 + xl, core]).astype(jnp.int32)
    vmem = pl.BlockSpec(memory_space=pltpu.VMEM)
    smem = pl.BlockSpec(memory_space=pltpu.SMEM)
    hbm = pl.BlockSpec(memory_space=pl.ANY)
    params = pltpu.CompilerParams(vmem_limit_bytes=VMEM_LIMIT)

    def all_to_all(x, axes):
        return lax.all_to_all(x, axes, split_axis=0, concat_axis=0, tiled=True)

    other = swap(screened, "core", 2, 1)

    trial = trial_vectors.reshape(4, 2, 16, 128).transpose(0, 2, 1, 3).reshape(128, 128)
    sent, block = pl.pallas_call(
        prepare_kernel,
        out_shape=[
            jax.ShapeDtypeStruct((8, 128 + 2 * NEAR, 128), BF),
            jax.ShapeDtypeStruct((160 - 2 * NEAR, 128), BF),
        ],
        in_specs=[vmem] * 3,
        out_specs=[vmem] * 2,
        compiler_params=pltpu.CompilerParams(vmem_limit_bytes=62 * 1024 * 1024),
        name="prepare",
    )(trial, cond_source, cond_target.transpose(0, 2, 1))
    near = all_to_all(sent, KT)

    sv = flip_if(core, val_source.reshape(4, 32, 8, 2, 4), 3).reshape(4, 32, 64)

    block = block[None]
    block = doubled(block, "y", 4, 1)
    block, sv = lax.optimization_barrier((block, sv))
    block = doubled(block, "y", 4, 3)
    block = doubled(block, X, 4, 1)[None]
    near, block = lax.optimization_barrier((near, block))

    pieces = pl.pallas_call(
        pair_kernel,
        out_shape=jax.ShapeDtypeStruct((8, TV + 16, 128), BF),
        in_specs=[vmem] * 3,
        out_specs=vmem,
        compiler_params=params,
        name="pairs",
    )(sv, near, val_target.reshape(16, 128))
    every = all_to_all(pieces, YX)

    block = doubled(block, "z", 4, 1)
    block = doubled(block, "z", 4, 3)
    far = swap(block, X, 4, 3)
    ct_near, ct_far = (swap(x[:, :, 128 - 2 * NEAR :], "core", 2, 1) for x in (block, far))

    zs = pl.pallas_call(
        screen_kernel,
        out_shape=jax.ShapeDtypeStruct((8, 16, 8, 128), BF),
        in_specs=[smem, smem, hbm, hbm] + [vmem] * 5,
        out_specs=vmem,
        scratch_shapes=[
            pltpu.VMEM((512, 4, 512), BF),
            pltpu.VMEM((512, 4, 512), BF),
            pltpu.VMEM((512, 2, 16, 128), BF),
            pltpu.VMEM((32, 2, 16, 16, 128), BF),
            pltpu.VMEM((16, 128, 512), F32),
            pltpu.VMEM((16, 128, 512), BF),
            pltpu.VMEM((512, 128), BF),
            pltpu.SemaphoreType.DMA((2,)),
        ],
        compiler_params=pltpu.CompilerParams(vmem_limit_bytes=24 * 1024 * 1024),
        cost_estimate=cost(8_000_000_000, 16_000_000),
        name="screen",
    )(me, pair_momentum, screened, other, every, block, far, ct_near, ct_far)

    tv = every[:, TV:]
    tv_other = swap(tv, "core", 2, 1).reshape(8, 2, 32, 32)
    tv = tv.reshape(8, 2, 32, 32)
    tv = jnp.where(core == 0, jnp.stack([tv, tv_other], axis=1), jnp.stack([tv_other, tv], axis=1))
    tv = tv.transpose(2, 3, 0, 1, 4).reshape(2, 32, 64, 2, 4)
    tv = jnp.stack([tv, jnp.flip(tv, 3)], axis=3).reshape(64, 1024)

    arrived = all_to_all(zs.reshape(128, 8, 128), ALL)
    result = jnp.dot(tv, arrived.reshape(1024, 128), preferred_element_type=F32)
    result = result.reshape(2, 32, 2, 64)
    result = jnp.stack([result[0, :, 0], result[1, :, 1]])
    return result.reshape(2, 1, 2048)


def solution(mesh):
    fine = Mesh(mesh.devices.reshape(2, 4, 4, 2, 2), ALL)
    kt, ks = ("xh", "z"), ("y", "xl", "core")
    in_specs = (
        P(kt, None, ks),
        P(kt, None, ks),
        P(ks, None, kt),
        P(ks, None, kt),
        P(ks, kt, None),
        P(None, kt + ks, None),
        P(),
    )
    return jax.shard_map(local, mesh=fine, in_specs=in_specs, out_specs=P(kt, ks, None), check_vma=False)
```

```python
import functools

import jax
import jax.numpy as jnp
from jax import lax
from jax.experimental import pallas as pl
from jax.experimental.pallas import tpu as pltpu
from jax.sharding import Mesh
from jax.sharding import PartitionSpec as P

ALL = ("xh", "z", "y", "xl", "core")
YX = ("y", "xl")
KT = ("xh", "z")
X = ("xh", "xl")
CHIPS = ("xh", "z", "y", "xl")
BF = jnp.bfloat16
F32 = jnp.float32
VMEM_LIMIT = 8 * 1024 * 1024
NEAR = 48
TV = 256 + 16 * NEAR


def swap(x, axes, size, mask):
    return lax.ppermute(x, axes, [(i, i ^ mask) for i in range(size)])


def flip_if(bit, x, axis):
    return jnp.where(bit == 1, jnp.flip(x, axis), x)


def doubled(x, axes, size, mask):
    return jnp.concatenate([x, swap(x, axes, size, mask)], axis=0)


def cost(flops, bytes_accessed):
    return pl.CostEstimate(flops=flops, bytes_accessed=bytes_accessed, transcendentals=0)


def prepare_kernel(trial_ref, cs_ref, ct_ref, sent_ref, block_ref):
    trial = trial_ref[...]
    for k in range(8):
        sent_ref[k, :128, :] = trial
    for sp in range(2):
        pair = jnp.concatenate([cs_ref[2 * sp], cs_ref[2 * sp + 1]], axis=0)
        turned = jnp.transpose(pair.astype(F32)).astype(BF)
        for k in range(8):
            sent_ref[k, 128 + sp * NEAR : 128 + (sp + 1) * NEAR, :] = turned[:NEAR]
        block_ref[sp * (64 - NEAR) : (sp + 1) * (64 - NEAR), :] = turned[NEAR:]
    block_ref[128 - 2 * NEAR :, :] = jnp.concatenate([ct_ref[0], ct_ref[1]], axis=1)


def pair_kernel(sv_ref, near_ref, tv_ref, out_hbm, out_ref, sems):
    for peer in range(8):
        for k in range(8):
            at = 256 + k * 2 * NEAR
            out_ref[peer, at : at + 2 * NEAR, :] = near_ref[k, 128 : 128 + 2 * NEAR]
        out_ref[peer, TV : TV + 16, :] = tv_ref[...]
    early = pltpu.make_async_copy(out_ref.at[:, 256:], out_hbm.at[:, 256:], sems.at[0])
    early.start()
    row = lax.broadcasted_iota(jnp.int32, (32, 32), 0)
    column = lax.broadcasted_iota(jnp.int32, (32, 32), 1)
    lane = lax.broadcasted_iota(jnp.int32, (32, 128), 1)
    parity = lax.broadcasted_iota(jnp.int32, (32, 128), 0) & 1
    mine = (lane >> 6) == parity
    factors = []
    for s in range(4):
        for odd in range(2):
            chosen = ((row >> 1) * 2 + odd == column).astype(F32).astype(BF)
            values = jnp.dot(chosen, sv_ref[s], preferred_element_type=F32)
            values = jnp.where(mine, jnp.concatenate([values, values], axis=1), 0.0)
            factors.append(jnp.transpose(values).astype(BF))
    low = lax.broadcasted_iota(jnp.int32, (128, 128), 1) < 64
    for k in range(8):
        for sp in range(2):
            parts = []
            for s in (2 * sp, 2 * sp + 1):
                block = near_ref[k, s * 32 : s * 32 + 32]
                parts += [jnp.dot(factors[2 * s + odd], block, preferred_element_type=F32) for odd in range(2)]
            crossed = pltpu.roll(jnp.where(low, parts[2], parts[1]), 64, 1)
            both = (jnp.where(low, parts[0], parts[3]) + crossed).reshape(2, 8, 8, 128)
            for peer in range(8):
                piece = jnp.concatenate([both[0, peer], both[1, peer]], axis=0)
                at = sp * 128 + k * 16
                out_ref[peer, at : at + 16, :] = piece.astype(BF)
    last = pltpu.make_async_copy(out_ref.at[:, :256], out_hbm.at[:, :256], sems.at[1])
    last.start()
    early.wait()
    last.wait()


def far_index(kt_mask, yx_mask):
    y_mask, xh_mask = yx_mask >> 1, kt_mask >> 2
    place = (((yx_mask & 1) ^ xh_mask) << 2) | (y_mask ^ (y_mask >> 1))
    return kt_mask ^ ((kt_mask >> 1) & 1), place


def chosen(near_ref, far_ref, j, i):
    return jnp.where(j < 4, near_ref[j & 3, i], far_ref[j & 3, i])


def screen_kernel(
    me_ref, pm_ref, own_ref, other_hbm, every_ref, near_ref, far_ref, ct_near_ref, ct_far_ref, out_ref,
    other_ref, w_ref, xs, acc, ys, ct, sems,
):
    here, yx_here, core = me_ref[0], me_ref[1], me_ref[2]
    pairs = ((other_hbm, other_ref),)
    fetches = [pltpu.make_async_copy(a, b, sems.at[i]) for i, (a, b) in enumerate(pairs)]
    for fetch in fetches:
        fetch.start()

    def eight_mats(step, carry):
        own, other = own_ref[pl.ds(step * 8, 8)], other_ref[pl.ds(step * 8, 8)]
        for half in range(2):
            parts = []
            for qb in (2 * half, 2 * half + 1):
                lanes = slice(qb * 128, qb * 128 + 128)
                parts += [own[:, :, lanes], other[:, :, lanes]]
            w_ref[pl.ds(step * 8, 8), half] = jnp.concatenate(parts, axis=1)
        return carry

    lane = lax.broadcasted_iota(jnp.int32, (128, 128), 1)
    first = lane < 64

    def one_chip(yx, carry):
        for sp in range(2):
            a = every_ref[yx, sp * 128 : sp * 128 + 128]
            none = jnp.zeros_like(a)
            lhs = jnp.concatenate([jnp.where(first, a, none), jnp.where(first, none, a)], axis=0)
            factors = []
            for kt in range(8):
                at = 256 + (kt * 2 + sp) * NEAR
                j, i = far_index(kt ^ here, yx ^ yx_here)
                rest = chosen(near_ref, far_ref, j, i)[sp * (64 - NEAR) : (sp + 1) * (64 - NEAR)]
                factors += [every_ref[yx, at : at + NEAR], rest]
            rhs = jnp.concatenate(factors, axis=0)
            x = lax.dot_general(lhs, rhs, (((1,), (1,)), ((), ())), preferred_element_type=F32)
            x = x.reshape(2, 16, 8, 512)
            for half in range(2):
                at = half * 256
                tile = jnp.concatenate([x[..., at : at + 128], x[..., at + 128 : at + 256]], axis=2)
                xs[pl.ds(yx * 4 + sp * 2, 2), half] = tile.astype(BF)
        return carry

    lax.fori_loop(0, 8, one_chip, 0)
    for fetch in fetches:
        fetch.wait()
    lax.fori_loop(0, 64, eight_mats, 0)
    for chunk in range(4):

        def one_target(t, carry, chunk=chunk):
            mats = []
            for yx in (2 * chunk, 2 * chunk + 1):
                source = (yx * 2 + core) * 4
                mats += [pm_ref[t, source + j] for j in range(4)]
            for half in range(2):
                w = [w_ref[m, half] for m in mats]
                for two in range(8):
                    sums = []
                    for n in (2 * two, 2 * two + 1):
                        terms = [w[j] * xs[chunk * 8 + j, half, n] for j in range(8)]
                        while len(terms) > 1:
                            terms = [terms[j] + terms[j + 1] for j in range(0, len(terms), 2)]
                        sums.append(terms[0].astype(F32))
                    rows = slice(two * 16, two * 16 + 16)
                    for qb in range(2):
                        lanes = slice(half * 256 + qb * 128, half * 256 + qb * 128 + 128)
                        part = jnp.concatenate([x[qb * 8 : qb * 8 + 8] for x in sums], axis=0)
                        if chunk > 0:
                            part = part + acc[t, rows, lanes]
                        if chunk < 3:
                            acc[t, rows, lanes] = part
                        else:
                            ys[t, rows, lanes] = part.astype(BF)
            return carry

        lax.fori_loop(0, 16, one_target, 0, unroll=4)

    def project(kt, carry):
        for yx in range(8):
            j, i = far_index(kt ^ here, yx ^ yx_here)
            ct[pl.ds(pl.multiple_of((yx * 2 + core) * 32, 32), 32), :] = chosen(near_ref, far_ref, j, i)[128 - 2 * NEAR :]
            sibling = chosen(ct_near_ref, ct_far_ref, j, i)
            ct[pl.ds(pl.multiple_of((yx * 2 + 1 - core) * 32, 32), 32), :] = sibling
        c = ct[...]
        z0 = jnp.dot(ys[2 * kt], c, preferred_element_type=F32)
        z1 = jnp.dot(ys[2 * kt + 1], c, preferred_element_type=F32)
        out_ref[kt] = jnp.where(first, z0, z1).reshape(16, 8, 128).astype(BF)
        return carry

    lax.fori_loop(0, 8, project, 0)


def local(val_target, cond_target, val_source, cond_source, trial_vectors, screened, pair_momentum):
    xh, z, y, xl, core = (lax.axis_index(a) for a in ALL)
    me = jnp.stack([xh * 4 + z, y * 2 + xl, core]).astype(jnp.int32)
    vmem = pl.BlockSpec(memory_space=pltpu.VMEM)
    smem = pl.BlockSpec(memory_space=pltpu.SMEM)
    hbm = pl.BlockSpec(memory_space=pl.ANY)
    params = pltpu.CompilerParams(vmem_limit_bytes=VMEM_LIMIT)

    def all_to_all(x, axes):
        return lax.all_to_all(x, axes, split_axis=0, concat_axis=0, tiled=True)

    other = swap(screened, "core", 2, 1)

    trial = trial_vectors.reshape(4, 2, 16, 128).transpose(0, 2, 1, 3).reshape(128, 128)
    sent, block = pl.pallas_call(
        prepare_kernel,
        out_shape=[
            jax.ShapeDtypeStruct((8, 128 + 2 * NEAR, 128), BF),
            jax.ShapeDtypeStruct((160 - 2 * NEAR, 128), BF),
        ],
        in_specs=[vmem] * 3,
        out_specs=[vmem] * 2,
        compiler_params=pltpu.CompilerParams(vmem_limit_bytes=62 * 1024 * 1024),
        name="prepare",
    )(trial, cond_source, cond_target.transpose(0, 2, 1))
    near = all_to_all(sent, KT)

    sv = flip_if(core, val_source.reshape(4, 32, 8, 2, 4), 3).reshape(4, 32, 64)

    block = block[None]
    block = doubled(block, "y", 4, 1)
    block, sv = lax.optimization_barrier((block, sv))
    block = doubled(block, "y", 4, 3)
    block = doubled(block, X, 4, 1)[None]
    near, block = lax.optimization_barrier((near, block))

    pieces = pl.pallas_call(
        pair_kernel,
        out_shape=jax.ShapeDtypeStruct((8, TV + 16, 128), BF),
        in_specs=[vmem] * 3,
        out_specs=hbm,
        scratch_shapes=[pltpu.VMEM((8, TV + 16, 128), BF), pltpu.SemaphoreType.DMA((2,))],
        compiler_params=params,
        name="pairs",
    )(sv, near, val_target.reshape(16, 128))
    every = all_to_all(pieces, YX)

    block = doubled(block, "z", 4, 1)
    block = doubled(block, "z", 4, 3)
    far = swap(block, X, 4, 3)
    ct_near, ct_far = (swap(x[:, :, 128 - 2 * NEAR :], "core", 2, 1) for x in (block, far))

    zs = pl.pallas_call(
        screen_kernel,
        out_shape=jax.ShapeDtypeStruct((8, 16, 8, 128), BF),
        in_specs=[smem, smem, vmem, hbm] + [vmem] * 5,
        out_specs=vmem,
        scratch_shapes=[
            pltpu.VMEM((512, 4, 512), BF),
            pltpu.VMEM((512, 2, 16, 128), BF),
            pltpu.VMEM((32, 2, 16, 16, 128), BF),
            pltpu.VMEM((16, 128, 512), F32),
            pltpu.VMEM((16, 128, 512), BF),
            pltpu.VMEM((512, 128), BF),
            pltpu.SemaphoreType.DMA((1,)),
        ],
        compiler_params=pltpu.CompilerParams(vmem_limit_bytes=24 * 1024 * 1024),
        cost_estimate=cost(8_000_000_000, 16_000_000),
        name="screen",
    )(me, pair_momentum, screened, other, every, block, far, ct_near, ct_far)

    tv = every[:, TV:]
    tv_other = swap(tv, "core", 2, 1).reshape(8, 2, 32, 32)
    tv = tv.reshape(8, 2, 32, 32)
    tv = jnp.where(core == 0, jnp.stack([tv, tv_other], axis=1), jnp.stack([tv_other, tv], axis=1))
    tv = tv.transpose(2, 3, 0, 1, 4).reshape(2, 32, 64, 2, 4)
    tv = jnp.stack([tv, jnp.flip(tv, 3)], axis=3).reshape(64, 1024)

    arrived = all_to_all(zs.reshape(128, 8, 128), ALL)
    result = jnp.dot(tv, arrived.reshape(1024, 128), preferred_element_type=F32)
    result = result.reshape(2, 32, 2, 64)
    result = jnp.stack([result[0, :, 0], result[1, :, 1]])
    return result.reshape(2, 1, 2048)


def solution(mesh):
    fine = Mesh(mesh.devices.reshape(2, 4, 4, 2, 2), ALL)
    kt, ks = ("xh", "z"), ("y", "xl", "core")
    in_specs = (
        P(kt, None, ks),
        P(kt, None, ks),
        P(ks, None, kt),
        P(ks, None, kt),
        P(ks, kt, None),
        P(None, kt + ks, None),
        P(),
    )
    return jax.shard_map(local, mesh=fine, in_specs=in_specs, out_specs=P(kt, ks, None), check_vma=False)
```

```python
import functools

import jax
import jax.numpy as jnp
from jax import lax
from jax.experimental import pallas as pl
from jax.experimental.pallas import tpu as pltpu
from jax.sharding import Mesh
from jax.sharding import PartitionSpec as P

ALL = ("xh", "z", "y", "xl", "core")
YX = ("y", "xl")
KT = ("xh", "z")
X = ("xh", "xl")
CHIPS = ("xh", "z", "y", "xl")
BF = jnp.bfloat16
F32 = jnp.float32
VMEM_LIMIT = 8 * 1024 * 1024
NEAR = 48
TV = 256 + 16 * NEAR


def swap(x, axes, size, mask):
    return lax.ppermute(x, axes, [(i, i ^ mask) for i in range(size)])


def flip_if(bit, x, axis):
    return jnp.where(bit == 1, jnp.flip(x, axis), x)


def doubled(x, axes, size, mask):
    return jnp.concatenate([x, swap(x, axes, size, mask)], axis=0)


def cost(flops, bytes_accessed):
    return pl.CostEstimate(flops=flops, bytes_accessed=bytes_accessed, transcendentals=0)


def prepare_kernel(trial_ref, cs_ref, ct_ref, sent_ref, block_ref):
    trial = trial_ref[...]
    for k in range(8):
        sent_ref[k, :128, :] = trial
    for sp in range(2):
        pair = jnp.concatenate([cs_ref[2 * sp], cs_ref[2 * sp + 1]], axis=0)
        turned = jnp.transpose(pair.astype(F32)).astype(BF)
        for k in range(8):
            sent_ref[k, 128 + sp * NEAR : 128 + (sp + 1) * NEAR, :] = turned[:NEAR]
        block_ref[sp * (64 - NEAR) : (sp + 1) * (64 - NEAR), :] = turned[NEAR:]
    block_ref[128 - 2 * NEAR :, :] = jnp.concatenate([ct_ref[0], ct_ref[1]], axis=1)


def pair_kernel(sv_ref, near_ref, tv_ref, out_hbm, out_ref, sems):
    for peer in range(8):
        for k in range(8):
            at = 256 + k * 2 * NEAR
            out_ref[peer, at : at + 2 * NEAR, :] = near_ref[k, 128 : 128 + 2 * NEAR]
        out_ref[peer, TV : TV + 16, :] = tv_ref[...]
    early = pltpu.make_async_copy(out_ref.at[:, 256:], out_hbm.at[:, 256:], sems.at[0])
    early.start()
    row = lax.broadcasted_iota(jnp.int32, (32, 32), 0)
    column = lax.broadcasted_iota(jnp.int32, (32, 32), 1)
    lane = lax.broadcasted_iota(jnp.int32, (32, 128), 1)
    parity = lax.broadcasted_iota(jnp.int32, (32, 128), 0) & 1
    mine = (lane >> 6) == parity
    factors = []
    for s in range(4):
        for odd in range(2):
            chosen = ((row >> 1) * 2 + odd == column).astype(F32).astype(BF)
            values = jnp.dot(chosen, sv_ref[s], preferred_element_type=F32)
            values = jnp.where(mine, jnp.concatenate([values, values], axis=1), 0.0)
            factors.append(jnp.transpose(values).astype(BF))
    low = lax.broadcasted_iota(jnp.int32, (128, 128), 1) < 64
    for k in range(8):
        for sp in range(2):
            parts = []
            for s in (2 * sp, 2 * sp + 1):
                block = near_ref[k, s * 32 : s * 32 + 32]
                parts += [jnp.dot(factors[2 * s + odd], block, preferred_element_type=F32) for odd in range(2)]
            crossed = pltpu.roll(jnp.where(low, parts[2], parts[1]), 64, 1)
            both = (jnp.where(low, parts[0], parts[3]) + crossed).reshape(2, 8, 8, 128)
            for peer in range(8):
                piece = jnp.concatenate([both[0, peer], both[1, peer]], axis=0)
                at = sp * 128 + k * 16
                out_ref[peer, at : at + 16, :] = piece.astype(BF)
    last = pltpu.make_async_copy(out_ref.at[:, :256], out_hbm.at[:, :256], sems.at[1])
    last.start()
    early.wait()
    last.wait()


def far_index(kt_mask, yx_mask):
    y_mask, xh_mask = yx_mask >> 1, kt_mask >> 2
    place = (((yx_mask & 1) ^ xh_mask) << 2) | (y_mask ^ (y_mask >> 1))
    return kt_mask ^ ((kt_mask >> 1) & 1), place


def chosen(near_ref, far_ref, j, i):
    return jnp.where(j < 4, near_ref[j & 3, i], far_ref[j & 3, i])


def screen_kernel(
    me_ref, pm_ref, own_ref, other_hbm, every_ref, near_ref, far_ref, ct_near_ref, ct_far_ref, out_ref,
    other_ref, w_ref, xs, acc, ys, sems,
):
    here, yx_here, core = me_ref[0], me_ref[1], me_ref[2]
    pairs = ((other_hbm, other_ref),)
    fetches = [pltpu.make_async_copy(a, b, sems.at[i]) for i, (a, b) in enumerate(pairs)]
    for fetch in fetches:
        fetch.start()

    def eight_mats(step, carry):
        own, other = own_ref[pl.ds(step * 8, 8)], other_ref[pl.ds(step * 8, 8)]
        for half in range(2):
            parts = []
            for qb in (2 * half, 2 * half + 1):
                lanes = slice(qb * 128, qb * 128 + 128)
                parts += [own[:, :, lanes], other[:, :, lanes]]
            w_ref[pl.ds(step * 8, 8), half] = jnp.concatenate(parts, axis=1)
        return carry

    lane = lax.broadcasted_iota(jnp.int32, (128, 128), 1)
    first = lane < 64

    def one_chip(yx, carry):
        for sp in range(2):
            a = every_ref[yx, sp * 128 : sp * 128 + 128]
            none = jnp.zeros_like(a)
            lhs = jnp.concatenate([jnp.where(first, a, none), jnp.where(first, none, a)], axis=0)
            factors = []
            for kt in range(8):
                at = 256 + (kt * 2 + sp) * NEAR
                j, i = far_index(kt ^ here, yx ^ yx_here)
                rest = chosen(near_ref, far_ref, j, i)[sp * (64 - NEAR) : (sp + 1) * (64 - NEAR)]
                factors += [every_ref[yx, at : at + NEAR], rest]
            rhs = jnp.concatenate(factors, axis=0)
            x = lax.dot_general(lhs, rhs, (((1,), (1,)), ((), ())), preferred_element_type=F32)
            x = x.reshape(2, 16, 8, 512)
            for half in range(2):
                at = half * 256
                tile = jnp.concatenate([x[..., at : at + 128], x[..., at + 128 : at + 256]], axis=2)
                xs[pl.ds(yx * 4 + sp * 2, 2), half] = tile.astype(BF)
        return carry

    lax.fori_loop(0, 8, one_chip, 0, unroll=4)
    for fetch in fetches:
        fetch.wait()
    lax.fori_loop(0, 64, eight_mats, 0)
    for chunk in range(4):

        def one_target(t, carry, chunk=chunk):
            mats = []
            for yx in (2 * chunk, 2 * chunk + 1):
                source = (yx * 2 + core) * 4
                mats += [pm_ref[t, source + j] for j in range(4)]
            for half in range(2):
                w = [w_ref[m, half] for m in mats]
                for two in range(8):
                    sums = []
                    for n in (2 * two, 2 * two + 1):
                        terms = [w[j] * xs[chunk * 8 + j, half, n] for j in range(8)]
                        while len(terms) > 1:
                            terms = [terms[j] + terms[j + 1] for j in range(0, len(terms), 2)]
                        sums.append(terms[0].astype(F32))
                    rows = slice(two * 16, two * 16 + 16)
                    for qb in range(2):
                        lanes = slice(half * 256 + qb * 128, half * 256 + qb * 128 + 128)
                        part = jnp.concatenate([x[qb * 8 : qb * 8 + 8] for x in sums], axis=0)
                        if chunk > 0:
                            part = part + acc[t, rows, lanes]
                        if chunk < 3:
                            acc[t, rows, lanes] = part
                        else:
                            ys[t, rows, lanes] = part.astype(BF)
            return carry

        lax.fori_loop(0, 16, one_target, 0, unroll=4)

    def project(kt, carry):
        parts = []
        for yx in range(8):
            j, i = far_index(kt ^ here, yx ^ yx_here)
            mine = chosen(near_ref, far_ref, j, i)[128 - 2 * NEAR :]
            sibling = chosen(ct_near_ref, ct_far_ref, j, i)
            parts += [jnp.where(core == 0, mine, sibling), jnp.where(core == 0, sibling, mine)]
        c = jnp.concatenate(parts, axis=0)
        z0 = jnp.dot(ys[2 * kt], c, preferred_element_type=F32)
        z1 = jnp.dot(ys[2 * kt + 1], c, preferred_element_type=F32)
        out_ref[kt] = jnp.where(first, z0, z1).reshape(16, 8, 128).astype(BF)
        return carry

    lax.fori_loop(0, 8, project, 0, unroll=4)


def local(val_target, cond_target, val_source, cond_source, trial_vectors, screened, pair_momentum):
    xh, z, y, xl, core = (lax.axis_index(a) for a in ALL)
    me = jnp.stack([xh * 4 + z, y * 2 + xl, core]).astype(jnp.int32)
    vmem = pl.BlockSpec(memory_space=pltpu.VMEM)
    smem = pl.BlockSpec(memory_space=pltpu.SMEM)
    hbm = pl.BlockSpec(memory_space=pl.ANY)
    params = pltpu.CompilerParams(vmem_limit_bytes=VMEM_LIMIT)

    def all_to_all(x, axes):
        return lax.all_to_all(x, axes, split_axis=0, concat_axis=0, tiled=True)

    other = swap(screened, "core", 2, 1)

    trial = trial_vectors.reshape(4, 2, 16, 128).transpose(0, 2, 1, 3).reshape(128, 128)
    sent, block = pl.pallas_call(
        prepare_kernel,
        out_shape=[
            jax.ShapeDtypeStruct((8, 128 + 2 * NEAR, 128), BF),
            jax.ShapeDtypeStruct((160 - 2 * NEAR, 128), BF),
        ],
        in_specs=[vmem] * 3,
        out_specs=[vmem] * 2,
        compiler_params=pltpu.CompilerParams(vmem_limit_bytes=62 * 1024 * 1024),
        name="prepare",
    )(trial, cond_source, cond_target.transpose(0, 2, 1))
    near = all_to_all(sent, KT)

    sv = flip_if(core, val_source.reshape(4, 32, 8, 2, 4), 3).reshape(4, 32, 64)

    block = block[None]
    block = doubled(block, "y", 4, 1)
    block, sv = lax.optimization_barrier((block, sv))
    block = doubled(block, "y", 4, 3)
    block = doubled(block, X, 4, 1)[None]
    near, block = lax.optimization_barrier((near, block))

    pieces = pl.pallas_call(
        pair_kernel,
        out_shape=jax.ShapeDtypeStruct((8, TV + 16, 128), BF),
        in_specs=[vmem] * 3,
        out_specs=hbm,
        scratch_shapes=[pltpu.VMEM((8, TV + 16, 128), BF), pltpu.SemaphoreType.DMA((2,))],
        compiler_params=params,
        name="pairs",
    )(sv, near, val_target.reshape(16, 128))
    every = all_to_all(pieces, YX)

    block = doubled(block, "z", 4, 1)
    block = doubled(block, "z", 4, 3)
    far = swap(block, X, 4, 3)
    ct_near, ct_far = (swap(x[:, :, 128 - 2 * NEAR :], "core", 2, 1) for x in (block, far))

    zs = pl.pallas_call(
        screen_kernel,
        out_shape=jax.ShapeDtypeStruct((8, 16, 8, 128), BF),
        in_specs=[smem, smem, vmem, hbm] + [vmem] * 5,
        out_specs=vmem,
        scratch_shapes=[
            pltpu.VMEM((512, 4, 512), BF),
            pltpu.VMEM((512, 2, 16, 128), BF),
            pltpu.VMEM((32, 2, 16, 16, 128), BF),
            pltpu.VMEM((16, 128, 512), F32),
            pltpu.VMEM((16, 128, 512), BF),
            pltpu.SemaphoreType.DMA((1,)),
        ],
        compiler_params=pltpu.CompilerParams(vmem_limit_bytes=24 * 1024 * 1024),
        cost_estimate=cost(8_000_000_000, 16_000_000),
        name="screen",
    )(me, pair_momentum, screened, other, every, block, far, ct_near, ct_far)

    tv = every[:, TV:]
    tv_other = swap(tv, "core", 2, 1).reshape(8, 2, 32, 32)
    tv = tv.reshape(8, 2, 32, 32)
    tv = jnp.where(core == 0, jnp.stack([tv, tv_other], axis=1), jnp.stack([tv_other, tv], axis=1))
    tv = tv.transpose(2, 3, 0, 1, 4).reshape(2, 32, 64, 2, 4)
    tv = jnp.stack([tv, jnp.flip(tv, 3)], axis=3).reshape(64, 1024)

    arrived = all_to_all(zs.reshape(128, 8, 128), ALL)
    result = jnp.dot(tv, arrived.reshape(1024, 128), preferred_element_type=F32)
    result = result.reshape(2, 32, 2, 64)
    result = jnp.stack([result[0, :, 0], result[1, :, 1]])
    return result.reshape(2, 1, 2048)


def solution(mesh):
    fine = Mesh(mesh.devices.reshape(2, 4, 4, 2, 2), ALL)
    kt, ks = ("xh", "z"), ("y", "xl", "core")
    in_specs = (
        P(kt, None, ks),
        P(kt, None, ks),
        P(ks, None, kt),
        P(ks, None, kt),
        P(ks, kt, None),
        P(None, kt + ks, None),
        P(),
    )
    return jax.shard_map(local, mesh=fine, in_specs=in_specs, out_specs=P(kt, ks, None), check_vma=False)
```

```python
import functools

import jax
import jax.numpy as jnp
from jax import lax
from jax.experimental import pallas as pl
from jax.experimental.pallas import tpu as pltpu
from jax.sharding import Mesh
from jax.sharding import PartitionSpec as P

ALL = ("xh", "z", "y", "xl", "core")
YX = ("y", "xl")
KT = ("xh", "z")
X = ("xh", "xl")
CHIPS = ("xh", "z", "y", "xl")
BF = jnp.bfloat16
F32 = jnp.float32
VMEM_LIMIT = 8 * 1024 * 1024
NEAR = 48
TV = 256 + 16 * NEAR


def swap(x, axes, size, mask):
    return lax.ppermute(x, axes, [(i, i ^ mask) for i in range(size)])


def flip_if(bit, x, axis):
    return jnp.where(bit == 1, jnp.flip(x, axis), x)


def doubled(x, axes, size, mask):
    return jnp.concatenate([x, swap(x, axes, size, mask)], axis=0)


def cost(flops, bytes_accessed):
    return pl.CostEstimate(flops=flops, bytes_accessed=bytes_accessed, transcendentals=0)


def prepare_kernel(trial_ref, cs_ref, ct_ref, sent_ref, block_ref):
    trial = trial_ref[...]
    for k in range(8):
        sent_ref[k, :128, :] = trial
    for sp in range(2):
        pair = jnp.concatenate([cs_ref[2 * sp], cs_ref[2 * sp + 1]], axis=0)
        turned = jnp.transpose(pair.astype(F32)).astype(BF)
        for k in range(8):
            sent_ref[k, 128 + sp * NEAR : 128 + (sp + 1) * NEAR, :] = turned[:NEAR]
        block_ref[sp * (64 - NEAR) : (sp + 1) * (64 - NEAR), :] = turned[NEAR:]
    block_ref[128 - 2 * NEAR :, :] = jnp.concatenate([ct_ref[0], ct_ref[1]], axis=1)


def pair_kernel(sv_ref, near_ref, tv_ref, out_hbm, out_ref, sems):
    for peer in range(8):
        for k in range(8):
            at = 256 + k * 2 * NEAR
            out_ref[peer, at : at + 2 * NEAR, :] = near_ref[k, 128 : 128 + 2 * NEAR]
        out_ref[peer, TV : TV + 16, :] = tv_ref[...]
    early = pltpu.make_async_copy(out_ref.at[:, 256:], out_hbm.at[:, 256:], sems.at[0])
    early.start()
    row = lax.broadcasted_iota(jnp.int32, (32, 32), 0)
    column = lax.broadcasted_iota(jnp.int32, (32, 32), 1)
    lane = lax.broadcasted_iota(jnp.int32, (32, 128), 1)
    parity = lax.broadcasted_iota(jnp.int32, (32, 128), 0) & 1
    mine = (lane >> 6) == parity
    factors = []
    for s in range(4):
        for odd in range(2):
            chosen = ((row >> 1) * 2 + odd == column).astype(F32).astype(BF)
            values = jnp.dot(chosen, sv_ref[s], preferred_element_type=F32)
            values = jnp.where(mine, jnp.concatenate([values, values], axis=1), 0.0)
            factors.append(jnp.transpose(values).astype(BF))
    low = lax.broadcasted_iota(jnp.int32, (128, 128), 1) < 64
    for k in range(8):
        for sp in range(2):
            parts = []
            for s in (2 * sp, 2 * sp + 1):
                block = near_ref[k, s * 32 : s * 32 + 32]
                parts += [jnp.dot(factors[2 * s + odd], block, preferred_element_type=F32) for odd in range(2)]
            crossed = pltpu.roll(jnp.where(low, parts[2], parts[1]), 64, 1)
            both = (jnp.where(low, parts[0], parts[3]) + crossed).reshape(2, 8, 8, 128)
            for peer in range(8):
                piece = jnp.concatenate([both[0, peer], both[1, peer]], axis=0)
                at = sp * 128 + k * 16
                out_ref[peer, at : at + 16, :] = piece.astype(BF)
    last = pltpu.make_async_copy(out_ref.at[:, :256], out_hbm.at[:, :256], sems.at[1])
    last.start()
    early.wait()
    last.wait()


def far_index(kt_mask, yx_mask):
    y_mask, xh_mask = yx_mask >> 1, kt_mask >> 2
    place = (((yx_mask & 1) ^ xh_mask) << 2) | (y_mask ^ (y_mask >> 1))
    return kt_mask ^ ((kt_mask >> 1) & 1), place


def chosen(near_ref, far_ref, j, i):
    return jnp.where(j < 4, near_ref[j & 3, i], far_ref[j & 3, i])


def screen_kernel(
    me_ref, pm_ref, own_ref, other_hbm, every_ref, near_ref, far_ref, ct_near_ref, ct_far_ref, out_ref,
    other_ref, w_ref, xs, acc, ys, sems,
):
    here, yx_here, core = me_ref[0], me_ref[1], me_ref[2]
    pairs = ((other_hbm, other_ref),)
    fetches = [pltpu.make_async_copy(a, b, sems.at[i]) for i, (a, b) in enumerate(pairs)]
    for fetch in fetches:
        fetch.start()

    def eight_mats(step, carry):
        own, other = own_ref[pl.ds(step * 8, 8)], other_ref[pl.ds(step * 8, 8)]
        for half in range(2):
            parts = []
            for qb in (2 * half, 2 * half + 1):
                lanes = slice(qb * 128, qb * 128 + 128)
                parts += [own[:, :, lanes], other[:, :, lanes]]
            w_ref[pl.ds(step * 8, 8), half] = jnp.concatenate(parts, axis=1)
        return carry

    lane = lax.broadcasted_iota(jnp.int32, (128, 128), 1)
    first = lane < 64

    def one_chip(yx, carry):
        for sp in range(2):
            a = every_ref[yx, sp * 128 : sp * 128 + 128]
            none = jnp.zeros_like(a)
            lhs = jnp.concatenate([jnp.where(first, a, none), jnp.where(first, none, a)], axis=0)
            factors = []
            for kt in range(8):
                at = 256 + (kt * 2 + sp) * NEAR
                j, i = far_index(kt ^ here, yx ^ yx_here)
                rest = chosen(near_ref, far_ref, j, i)[sp * (64 - NEAR) : (sp + 1) * (64 - NEAR)]
                factors += [every_ref[yx, at : at + NEAR], rest]
            rhs = jnp.concatenate(factors, axis=0)
            x = lax.dot_general(lhs, rhs, (((1,), (1,)), ((), ())), preferred_element_type=F32)
            x = x.reshape(2, 16, 8, 512)
            for half in range(2):
                at = half * 256
                tile = jnp.concatenate([x[..., at : at + 128], x[..., at + 128 : at + 256]], axis=2)
                xs[pl.ds(yx * 4 + sp * 2, 2), half] = tile.astype(BF)
        return carry

    lax.fori_loop(0, 8, one_chip, 0, unroll=4)
    for fetch in fetches:
        fetch.wait()
    lax.fori_loop(0, 64, eight_mats, 0, unroll=8)
    for chunk in range(4):

        def one_target(t, carry, chunk=chunk):
            mats = []
            for yx in (2 * chunk, 2 * chunk + 1):
                source = (yx * 2 + core) * 4
                mats += [pm_ref[t, source + j] for j in range(4)]
            for half in range(2):
                w = [w_ref[m, half] for m in mats]
                for two in range(8):
                    sums = []
                    for n in (2 * two, 2 * two + 1):
                        terms = [w[j] * xs[chunk * 8 + j, half, n] for j in range(8)]
                        while len(terms) > 1:
                            terms = [terms[j] + terms[j + 1] for j in range(0, len(terms), 2)]
                        sums.append(terms[0].astype(F32))
                    rows = slice(two * 16, two * 16 + 16)
                    for qb in range(2):
                        lanes = slice(half * 256 + qb * 128, half * 256 + qb * 128 + 128)
                        part = jnp.concatenate([x[qb * 8 : qb * 8 + 8] for x in sums], axis=0)
                        if chunk > 0:
                            part = part + acc[t, rows, lanes]
                        if chunk < 3:
                            acc[t, rows, lanes] = part
                        else:
                            ys[t, rows, lanes] = part.astype(BF)
            return carry

        lax.fori_loop(0, 16, one_target, 0, unroll=4)

    def project(kt, carry):
        parts = []
        for yx in range(8):
            j, i = far_index(kt ^ here, yx ^ yx_here)
            mine = chosen(near_ref, far_ref, j, i)[128 - 2 * NEAR :]
            sibling = chosen(ct_near_ref, ct_far_ref, j, i)
            parts += [jnp.where(core == 0, mine, sibling), jnp.where(core == 0, sibling, mine)]
        c = jnp.concatenate(parts, axis=0)
        z0 = jnp.dot(ys[2 * kt], c, preferred_element_type=F32)
        z1 = jnp.dot(ys[2 * kt + 1], c, preferred_element_type=F32)
        out_ref[kt] = jnp.where(first, z0, z1).reshape(16, 8, 128).astype(BF)
        return carry

    lax.fori_loop(0, 8, project, 0, unroll=4)


def local(val_target, cond_target, val_source, cond_source, trial_vectors, screened, pair_momentum):
    xh, z, y, xl, core = (lax.axis_index(a) for a in ALL)
    me = jnp.stack([xh * 4 + z, y * 2 + xl, core]).astype(jnp.int32)
    vmem = pl.BlockSpec(memory_space=pltpu.VMEM)
    smem = pl.BlockSpec(memory_space=pltpu.SMEM)
    hbm = pl.BlockSpec(memory_space=pl.ANY)
    params = pltpu.CompilerParams(vmem_limit_bytes=VMEM_LIMIT)

    def all_to_all(x, axes):
        return lax.all_to_all(x, axes, split_axis=0, concat_axis=0, tiled=True)

    other = swap(screened, "core", 2, 1)

    trial = trial_vectors.reshape(4, 2, 16, 128).transpose(0, 2, 1, 3).reshape(128, 128)
    sent, block = pl.pallas_call(
        prepare_kernel,
        out_shape=[
            jax.ShapeDtypeStruct((8, 128 + 2 * NEAR, 128), BF),
            jax.ShapeDtypeStruct((160 - 2 * NEAR, 128), BF),
        ],
        in_specs=[vmem] * 3,
        out_specs=[vmem] * 2,
        compiler_params=pltpu.CompilerParams(vmem_limit_bytes=62 * 1024 * 1024),
        name="prepare",
    )(trial, cond_source, cond_target.transpose(0, 2, 1))
    near = all_to_all(sent, KT)

    sv = flip_if(core, val_source.reshape(4, 32, 8, 2, 4), 3).reshape(4, 32, 64)

    block = block[None]
    block = doubled(block, "y", 4, 1)
    block, sv = lax.optimization_barrier((block, sv))
    block = doubled(block, "y", 4, 3)
    block = doubled(block, X, 4, 1)[None]
    near, block = lax.optimization_barrier((near, block))

    pieces = pl.pallas_call(
        pair_kernel,
        out_shape=jax.ShapeDtypeStruct((8, TV + 16, 128), BF),
        in_specs=[vmem] * 3,
        out_specs=hbm,
        scratch_shapes=[pltpu.VMEM((8, TV + 16, 128), BF), pltpu.SemaphoreType.DMA((2,))],
        compiler_params=params,
        name="pairs",
    )(sv, near, val_target.reshape(16, 128))
    every = all_to_all(pieces, YX)

    block = doubled(block, "z", 4, 1)
    block = doubled(block, "z", 4, 3)
    far = swap(block, X, 4, 3)
    ct_near, ct_far = (swap(x[:, :, 128 - 2 * NEAR :], "core", 2, 1) for x in (block, far))

    zs = pl.pallas_call(
        screen_kernel,
        out_shape=jax.ShapeDtypeStruct((8, 16, 8, 128), BF),
        in_specs=[smem, smem, vmem, hbm] + [vmem] * 5,
        out_specs=vmem,
        scratch_shapes=[
            pltpu.VMEM((512, 4, 512), BF),
            pltpu.VMEM((512, 2, 16, 128), BF),
            pltpu.VMEM((32, 2, 16, 16, 128), BF),
            pltpu.VMEM((16, 128, 512), F32),
            pltpu.VMEM((16, 128, 512), BF),
            pltpu.SemaphoreType.DMA((1,)),
        ],
        compiler_params=pltpu.CompilerParams(vmem_limit_bytes=24 * 1024 * 1024),
        cost_estimate=cost(8_000_000_000, 16_000_000),
        name="screen",
    )(me, pair_momentum, screened, other, every, block, far, ct_near, ct_far)

    tv = every[:, TV:]
    tv_other = swap(tv, "core", 2, 1).reshape(8, 2, 32, 32)
    tv = tv.reshape(8, 2, 32, 32)
    tv = jnp.where(core == 0, jnp.stack([tv, tv_other], axis=1), jnp.stack([tv_other, tv], axis=1))
    tv = tv.transpose(2, 3, 0, 1, 4).reshape(2, 32, 64, 2, 4)
    tv = jnp.stack([tv, jnp.flip(tv, 3)], axis=3).reshape(64, 1024)

    arrived = all_to_all(zs.reshape(128, 8, 128), ALL)
    result = jnp.dot(tv, arrived.reshape(1024, 128), preferred_element_type=F32)
    result = result.reshape(2, 32, 2, 64)
    result = jnp.stack([result[0, :, 0], result[1, :, 1]])
    return result.reshape(2, 1, 2048)


def solution(mesh):
    fine = Mesh(mesh.devices.reshape(2, 4, 4, 2, 2), ALL)
    kt, ks = ("xh", "z"), ("y", "xl", "core")
    in_specs = (
        P(kt, None, ks),
        P(kt, None, ks),
        P(ks, None, kt),
        P(ks, None, kt),
        P(ks, kt, None),
        P(None, kt + ks, None),
        P(),
    )
    return jax.shard_map(local, mesh=fine, in_specs=in_specs, out_specs=P(kt, ks, None), check_vma=False)
```
